32 devices in a mesh: db: 8 (over y, x, core), pb: 4 (over z).
Axes of the slice: x: 2, y: 2, z: 4, core: 2. Of those that a mesh axis runs over, the one named last changes fastest.
Arguments:
- query_maps: bfloat16 [32, 256, 256], P(('db', 'pb')), may hold values from -6 to 6
- database: bfloat16 [1024, 256, 256], P(('db', 'pb')), may hold values from -6 to 6
- shortlist: int32 [32, 128], P(('db', 'pb')), may hold values from 0 to 1023, as said below
- kernel_query: bfloat16 [3, 3], replicated, may hold values from -1.5 to 1.5
- kernel_db: bfloat16 [3, 3], replicated, may hold values from -1.5 to 1.5
Outputs:
- scores: float32 [32, 128], P(('db', 'pb'))
- top_scores: float32 [32, 100], P(('db', 'pb'))
The draws below stay inside these ranges and needn't reach their ends.
Inputs may be any that keep to these rules, and one draw needn't show every extreme that they name: Within one query the ids are distinct. Among the 128 shortlist entries of the query held by device q (query q), at most 8 lie in any one shard of images (ids s * 32 to (s + 1) * 32 - 1), and some shard holds exactly 8 of them for every device.
All inputs are finite; a program needn't handle non-finite values.
Results may differ from the reference program's by a relative error of at most 0.0003.
Values may be sent and summed in bfloat16 or wider, within the bound.
A program may use at most 128 MiB of HBM per device.

```python
import jax
import jax.numpy as jnp
from jax import lax

C = 256
GRID = 16
CAND = 128
TOPK = 100
Q_DEV = 1
IMG_DEV = 32
NQ = 32
DB_IMG = 1024
CAP = 8


def draw_shortlist(key, part):
    shard_count = DB_IMG // IMG_DEV
    block_count = NQ // Q_DEV
    entry_count = shard_count * CAP
    take_count = Q_DEV * CAND
    hottest = jax.random.randint(jax.random.fold_in(key, 11), (), 0, shard_count)

    def one_slots(slot_key):
        return jax.random.permutation(slot_key, IMG_DEV)[:CAP]

    def one_block(block_key):
        first_key, second_key, third_key = jax.random.split(block_key, 3)
        order = jax.random.permutation(first_key, entry_count)
        shard_entry = jnp.arange(entry_count) // CAP
        priority = order + jnp.where(shard_entry == hottest, -entry_count, 0)
        chosen = jnp.argsort(priority)[:take_count]
        chosen = chosen[jax.random.permutation(second_key, take_count)]
        shard_pick = chosen // CAP
        within = chosen % CAP
        slot_table = jax.vmap(one_slots)(jax.random.split(third_key, shard_count))
        image_ids = shard_pick * IMG_DEV + slot_table[shard_pick, within]
        return image_ids.reshape(Q_DEV, CAND)
    block_keys = jax.random.split(jax.random.fold_in(key, 12), block_count)
    return jax.vmap(one_block)(block_keys).reshape(NQ, CAND).astype(jnp.int32)


def levels(key, shape, shards, smallest, high):
    factor_of = 1.0
    for position, blocks in shards:
        heights = jax.random.uniform(jax.random.fold_in(jax.random.fold_in(key, 6), position), (blocks,), jnp.float32, smallest / len(shards), high / len(shards))
        factor_of = factor_of * jnp.repeat(jnp.exp(heights), shape[position] // blocks).reshape((-1,) + (1,) * (len(shape) - 1 - position))
    return factor_of


def bell_draw(key, dims, spread, reach, cuts=(), kind=jnp.bfloat16):
    array = jax.random.normal(key, dims, jnp.float32) * spread
    if len(cuts) > 0:
        array = levels(key, dims, cuts, -0.22, 0.18) * array
    return jnp.clip(array, min=-reach, max=reach).astype(kind)


def setup_inputs(seed: int = 0) -> dict:
    streams_of = jax.random.split(jax.random.key(seed), 6)
    query_maps = bell_draw(streams_of[0], (NQ, C, GRID * GRID), 1.0, 6.0, ((0, 32),))
    database = bell_draw(streams_of[1], (DB_IMG, C, GRID * GRID), 1.0, 6.0, ((0, 32),))
    shortlist = draw_shortlist(jax.random.fold_in(streams_of[5], 71), 0)
    kernel_query = bell_draw(streams_of[3], (3, 3), 0.33, 1.5)
    kernel_db = bell_draw(streams_of[4], (3, 3), 0.33, 1.5)
    return {"query_maps": query_maps, "database": database, "shortlist": shortlist, "kernel_query": kernel_query, "kernel_db": kernel_db}


epsilon = 1e-06
score_scale = 8.0

def unit_maps(maps):
    values = maps.astype(jnp.float32)
    squares = lax.optimization_barrier(jnp.sum(values * values, axis=1, keepdims=True))
    return (values * lax.rsqrt(squares + epsilon)).astype(jnp.bfloat16)

def reference(query_maps, database, shortlist, kernel_query, kernel_db):
    query_unit = unit_maps(query_maps)
    taps_query = kernel_query.astype(jnp.float32)
    taps_db = kernel_db.astype(jnp.float32)

    def per_query(inputs):
        query_one, image_ids = inputs
        images = unit_maps(database[image_ids.astype(jnp.int32)])
        correlation = jnp.einsum('cq,ncd->nqd', query_one.astype(jnp.float32), images.astype(jnp.float32))
        rectified = jnp.maximum(correlation, 0.0).astype(jnp.bfloat16)
        rectified = lax.optimization_barrier(rectified).astype(jnp.float32)
        grid_form = rectified.reshape(CAND, GRID, GRID, GRID, GRID)
        pad_query = jnp.pad(grid_form, ((0, 0), (1, 1), (1, 1), (0, 0), (0, 0)))
        pad_db = jnp.pad(grid_form, ((0, 0), (0, 0), (0, 0), (1, 1), (1, 1)))
        filtered = jnp.zeros_like(grid_form)
        for i in range(3):
            for j in range(3):
                filtered = filtered + taps_query[i, j] * pad_query[:, i:i + GRID, j:j + GRID, :, :]
                filtered = filtered + taps_db[i, j] * pad_db[:, :, :, i:i + GRID, j:j + GRID]
        filtered = filtered.reshape(CAND, GRID * GRID, GRID * GRID)
        return score_scale * lax.optimization_barrier(jnp.mean(lax.optimization_barrier(jnp.max(filtered, axis=1)), axis=-1))
    scores = lax.map(per_query, (query_unit, shortlist))
    top_scores = lax.top_k(scores, TOPK)[0]
    return (scores, top_scores)
```

```python
import functools
import math

import jax
import jax.numpy as jnp
from jax import lax
from jax.experimental import pallas as pl
from jax.experimental.pallas import tpu as pltpu
from jax.sharding import PartitionSpec as P

GRID = 16
TOPK = 100
LANES = 128
ROWS = 8
TAIL = 16
EARLY = 2
MESH = pl.DeviceIdType.MESH

epsilon = 1e-06
score_scale = 8.0


def unit_map(values):
    squares = jnp.sum(values * values, axis=0, keepdims=True)
    return values * lax.rsqrt(squares + epsilon)


def fill_filters(query_taps, db_taps, filter_query, filter_db):
    cells = filter_query.shape[0]
    row = lax.broadcasted_iota(jnp.int32, (cells, cells), 0)
    col = lax.broadcasted_iota(jnp.int32, (cells, cells), 1)
    down = (col >> 4) - (row >> 4)
    across = (col & (GRID - 1)) - (row & (GRID - 1))
    near = (jnp.abs(down) <= 1) & (jnp.abs(across) <= 1)
    tap = jnp.where(near, down * 3 + across + 4, -1)
    query_matrix = jnp.zeros((cells, cells), jnp.float32)
    db_matrix = jnp.zeros((cells, cells), jnp.float32)
    query_values = query_taps[...].astype(jnp.float32)
    db_values = db_taps[...].astype(jnp.float32)
    for i in range(3):
        for j in range(3):
            hit = tap == 3 * i + j
            back = tap == 8 - (3 * i + j)
            query_matrix = jnp.where(hit, query_values[i : i + 1, j : j + 1], query_matrix)
            db_matrix = jnp.where(back, db_values[i : i + 1, j : j + 1], db_matrix)
    filter_query[...] = query_matrix.astype(jnp.bfloat16)
    filter_db[...] = db_matrix.astype(jnp.bfloat16)


def shortlist_info(ids, image_count, count):
    entries = ids.shape[1]
    shard = jnp.zeros_like(ids)
    for s in range(1, count):
        shard = shard + jnp.where(ids >= s * image_count, 1, 0)
    slot = ids - shard * image_count
    across = jnp.broadcast_to(shard, (entries, entries))
    above = lax.broadcasted_iota(jnp.int32, (entries, entries), 0)
    beside = lax.broadcasted_iota(jnp.int32, (entries, entries), 1)
    earlier = (across.T == across) & (above < beside)
    bucket = jnp.sum(jnp.where(earlier, 1, 0), axis=0, keepdims=True)
    rank = lax.broadcasted_iota(jnp.int32, (TAIL, entries), 0)
    return jnp.where(rank == 0, shard, jnp.where(rank == 1, slot, bucket))


def descending(row):
    entries = row.shape[1]
    across = jnp.broadcast_to(row, (entries, entries))
    down = across.T
    above = lax.broadcasted_iota(jnp.int32, (entries, entries), 0)
    beside = lax.broadcasted_iota(jnp.int32, (entries, entries), 1)
    ahead = (down > across) | ((down == across) & (above < beside))
    rank = jnp.sum(jnp.where(ahead, 1.0, 0.0), axis=0, keepdims=True)
    rank_down = jnp.broadcast_to(rank, (entries, entries)).T
    chosen = jnp.where(rank_down == beside.astype(jnp.float32), down, 0.0)
    return jnp.sum(chosen, axis=0, keepdims=True)


def flip(a, b, size):
    total = 0
    bit = 1
    while bit < size:
        total = total + lax.rem(a // bit + b // bit, 2) * bit
        bit *= 2
    return total


def combo_order(side, line):
    order = []
    for wave in range(line + 2):
        for v in range(side):
            for u in range(side):
                j = wave - min(u, 1) - min(v, 1)
                if 0 <= j < line:
                    order.append((j * side + u) * side + v)
    return order


def kernel(
    db_count,
    pb_count,
    width,
    query_any,
    shortlist_ref,
    database_ref,
    query_taps,
    db_taps,
    out_ref,
    sorted_ref,
    filter_query,
    filter_db,
    raw,
    positive,
    maps,
    info,
    units,
    slot_rows,
    slot_table,
    peaks,
    found,
    returned,
    query_ref,
    map_send,
    map_recv,
    back_send,
    back_recv,
    slot_sem,
    raw_sem,
    query_sem,
):
    count = db_count * pb_count
    chips = db_count // 2
    side = math.isqrt(chips)
    combos = pb_count * chips
    order = combo_order(side, pb_count)
    image_count = database_ref.shape[0]
    cells = units.shape[2]
    db = lax.axis_index("db")
    pb = lax.axis_index("pb")
    chip = db // 2
    core = lax.rem(db, 2)
    me = db * pb_count + pb
    partner = (chip * 2 + 1 - core, pb)
    first_stride = 1 + core * (side - 1)
    second_stride = side - core * (side - 1)

    first_base = pb_count - 1
    second_base = first_base + pb_count * (side - 1)
    partner_base = second_base + pb_count * side * (side - 1)
    sends = partner_base + combos

    def place(index):
        return (index // pb_count, lax.rem(index, pb_count))

    def line_peer(j):
        return (db, flip(pb, j, pb_count))

    def first_peer(u):
        return (flip(chip, u * first_stride, chips) * 2 + core, pb)

    def second_peer(v):
        return (flip(chip, v * second_stride, chips) * 2 + core, pb)

    def map_copy(source, send_slot, device):
        return pltpu.make_async_remote_copy(
            src_ref=maps.at[source],
            dst_ref=maps.at[source],
            send_sem=map_send.at[send_slot],
            recv_sem=map_recv.at[source],
            device_id=device,
            device_id_type=MESH,
        )

    def send_first(source, j):
        for u in range(1, side):
            map_copy(source, first_base + j * (side - 1) + u - 1, first_peer(u)).start()

    def send_second(source, j, u):
        for v in range(1, side):
            slot = second_base + (j * side + u) * (side - 1) + v - 1
            map_copy(source, slot, second_peer(v)).start()

    def back_copy(source, landed):
        return pltpu.make_async_remote_copy(
            src_ref=found.at[source],
            dst_ref=returned.at[landed],
            send_sem=back_send.at[source],
            recv_sem=back_recv.at[landed],
            device_id=place(source),
            device_id_type=MESH,
        )

    def raw_copy(image):
        return pltpu.make_async_copy(database_ref.at[image], raw.at[image], raw_sem.at[image])

    def slot_copy(parity):
        return pltpu.make_async_copy(
            slot_rows.at[parity], slot_table.at[parity], slot_sem.at[parity]
        )

    barrier = pltpu.get_barrier_semaphore()
    peers = [line_peer(j) for j in range(1, pb_count)]
    peers += [first_peer(u) for u in range(1, side)]
    peers += [second_peer(v) for v in range(1, side)]
    peers += [partner]
    for peer in peers:
        pl.semaphore_signal(barrier, inc=1, device_id=peer, device_id_type=MESH)

    query_copy = pltpu.make_async_copy(query_any.at[0], query_ref, query_sem)
    query_copy.start()

    @pl.loop(0, image_count)
    def _(image):
        raw_copy(image).start()

    my_info = shortlist_info(shortlist_ref[...], image_count, count)
    info[...] = my_info
    entries = my_info.shape[1]
    maps[me, cells : cells + TAIL, 0:entries] = my_info.astype(jnp.float32).astype(jnp.bfloat16)
    if maps.shape[2] > entries:
        maps[me, cells : cells + TAIL, entries:] = jnp.zeros(
            (TAIL, maps.shape[2] - entries), jnp.bfloat16
        )
    query_copy.wait()
    maps[me, 0:cells, :] = unit_map(query_ref[...].astype(jnp.float32)).T.astype(jnp.bfloat16)
    rank = lax.broadcasted_iota(jnp.int32, (ROWS, entries), 0)
    rank_value = rank.astype(jnp.float32)
    me_value = jnp.full((ROWS, entries), me, jnp.int32).astype(jnp.float32)

    def normalize(image):
        raw_copy(image).wait()
        units[image] = unit_map(raw[image].astype(jnp.float32)).astype(jnp.bfloat16)

    early = image_count // EARLY
    pl.loop(0, early)(normalize)
    pl.semaphore_wait(barrier, len(peers))

    send_first(me, 0)
    for j in range(1, pb_count):
        map_copy(me, j - 1, line_peer(j)).start()
    map_copy(me, partner_base, partner).start()

    fill_filters(query_taps, db_taps, filter_query, filter_db)
    peaks[...] = jnp.zeros_like(peaks)
    pl.loop(early, image_count)(normalize)

    def decode(turn):
        last = 2 * combos - 1
        odd = lax.rem(turn, 2)
        mid = jnp.where(odd == 1, (turn + 1) // 2, turn // 2 - 1)
        index = jnp.where(turn < 2, 0, jnp.where(turn == 2, 1, mid))
        index = jnp.where(turn == last, combos - 1, index)
        half = jnp.where((turn == 1) | (turn == last), 1, jnp.where(turn < 4, 0, 1 - odd))
        code = 0
        for n in range(combos):
            code = jnp.where(index == n, order[n], code)
        j = code // chips
        u = lax.rem(code // side, side)
        v = lax.rem(code, side)
        owner = lax.rem(core + half, 2)
        offset = u * (1 + owner * (side - 1)) + v * (side - owner * (side - 1))
        other_chip = flip(chip, offset, chips)
        source = (other_chip * 2 + owner) * pb_count + flip(pb, j, pb_count)
        return half, code, j, u, v, source

    def load_slots(source, parity):
        tail = maps[source, cells : cells + TAIL, 0:entries].astype(jnp.float32)
        hit = (tail[0:1, :] == me_value) & (tail[2:3, :] == rank_value)
        slot = jnp.sum(jnp.where(hit, tail[1:2, :], 0.0), axis=1, keepdims=True)
        slot_rows[parity] = jnp.broadcast_to(slot, (ROWS, entries)).astype(jnp.int32)
        slot_copy(parity).start()

    def serve(turn, half, code, j, u, v, source):
        map_copy(source, 0, partner).wait_recv()

        @pl.when(half == 0)
        def _():
            map_copy(source, partner_base + code, partner).start()

            @pl.when((u == 0) & (v == 0))
            def _():
                send_first(source, j)

            @pl.when(v == 0)
            def _():
                send_second(source, j, u)

        @pl.when(turn == 1)
        def _():
            send_second(me, 0, 0)

        load_slots(source, lax.rem(turn, 2))

    load_slots(me, 0)

    def step(turn, source):
        parity = lax.rem(turn, 2)
        coming = decode(turn + 1)
        upcoming = coming[-1]

        @pl.when((turn >= 3) & (turn + 1 < 2 * combos))
        def _():
            serve(turn + 1, *coming)

        slot_copy(parity).wait()
        for k in range(width):
            slot = jnp.clip(slot_table[parity, k, 0], 0, image_count - 1)
            correlation = jnp.dot(
                maps[source, 0:cells, :], units[slot], preferred_element_type=jnp.float32
            )
            positive[k] = jnp.maximum(correlation, 0.0).astype(jnp.bfloat16)
        for k in range(width):
            rectified = positive[k]
            filtered = jnp.dot(
                filter_query[...], rectified, preferred_element_type=jnp.float32
            ) + jnp.dot(rectified, filter_db[...], preferred_element_type=jnp.float32)
            peaks[k : k + 1, :] = jnp.max(filtered, axis=0, keepdims=True)
        best = peaks[...]
        total = jnp.sum(best, axis=1, keepdims=True) * (score_scale / best.shape[1])
        found[source] = jnp.broadcast_to(total, (ROWS, LANES))

        @pl.when(source != me)
        def _():
            back_copy(source, me).start()

        @pl.when(turn < 3)
        def _():
            serve(turn + 1, *coming)

        return upcoming

    lax.fori_loop(0, 2 * combos, step, me)

    returned[me] = found[me]

    @pl.loop(1, count)
    def _(step):
        other = lax.rem(me + step, count)
        back_copy(other, other).wait_recv()

    my_shard = info[0:1, :]
    my_bucket = info[2:3, :]
    scores = jnp.zeros((ROWS, LANES), jnp.float32)
    for s in range(count):
        scores = scores + jnp.where((my_shard == s) & (my_bucket == rank), returned[s], 0.0)
    final = jnp.sum(scores, axis=0, keepdims=True)
    out_ref[...] = final
    sorted_ref[...] = descending(final)

    @pl.loop(1, count)
    def _(step):
        back_copy(lax.rem(me + step, count), me).wait_send()

    @pl.loop(0, sends)
    def _(slot):
        map_copy(me, slot, partner).wait_send()


def body(db_count, pb_count, query_maps, database, shortlist, kernel_query, kernel_db):
    count = db_count * pb_count
    chips = db_count // 2
    side = math.isqrt(chips)
    sends = pb_count - 1 + pb_count * (side - 1) * (1 + side) + pb_count * chips
    image_count, channels, cells = database.shape
    entries = shortlist.shape[1]
    width = 2 * entries // count
    vmem = pl.BlockSpec(memory_space=pltpu.VMEM)
    whole = pl.BlockSpec(memory_space=pl.ANY)
    row = jax.ShapeDtypeStruct((1, entries), jnp.float32)
    scores, ordered = pl.pallas_call(
        functools.partial(kernel, db_count, pb_count, width),
        out_shape=(row, row),
        in_specs=[whole, vmem, whole, vmem, vmem],
        out_specs=(vmem, vmem),
        scratch_shapes=[
            pltpu.VMEM((cells, cells), jnp.bfloat16),
            pltpu.VMEM((cells, cells), jnp.bfloat16),
            pltpu.VMEM((image_count, channels, cells), jnp.bfloat16),
            pltpu.VMEM((width, cells, cells), jnp.bfloat16),
            pltpu.VMEM((count, cells + TAIL, channels), jnp.bfloat16),
            pltpu.VMEM((TAIL, entries), jnp.int32),
            pltpu.VMEM((image_count, channels, cells), jnp.bfloat16),
            pltpu.VMEM((2, ROWS, entries), jnp.int32),
            pltpu.SMEM((2, ROWS, entries), jnp.int32),
            pltpu.VMEM((ROWS, cells), jnp.float32),
            pltpu.VMEM((count, ROWS, LANES), jnp.float32),
            pltpu.VMEM((count, ROWS, LANES), jnp.float32),
            pltpu.VMEM((channels, cells), jnp.bfloat16),
            pltpu.SemaphoreType.DMA((sends,)),
            pltpu.SemaphoreType.DMA((count,)),
            pltpu.SemaphoreType.DMA((count,)),
            pltpu.SemaphoreType.DMA((count,)),
            pltpu.SemaphoreType.DMA((2,)),
            pltpu.SemaphoreType.DMA((image_count,)),
            pltpu.SemaphoreType.DMA,
        ],
        compiler_params=pltpu.CompilerParams(
            collective_id=0, has_side_effects=True, vmem_limit_bytes=56 * 1024 * 1024
        ),
    )(query_maps, shortlist, database, kernel_query, kernel_db)
    return (scores, ordered[:, :TOPK])


def solution(mesh):
    in_specs = (
        P(("db", "pb"), None, None),
        P(("db", "pb"), None, None),
        P(("db", "pb"), None),
        P(),
        P(),
    )
    out_specs = (P(("db", "pb"), None), P(("db", "pb"), None))
    step = functools.partial(body, mesh.shape["db"], mesh.shape["pb"])
    return jax.shard_map(step, mesh=mesh, in_specs=in_specs, out_specs=out_specs, check_vma=False)
```

```python
import functools
import math

import jax
import jax.numpy as jnp
from jax import lax
from jax.experimental import pallas as pl
from jax.experimental.pallas import tpu as pltpu
from jax.sharding import PartitionSpec as P

GRID = 16
TOPK = 100
LANES = 128
ROWS = 8
TAIL = 16
EARLY = 2
MESH = pl.DeviceIdType.MESH

epsilon = 1e-06
score_scale = 8.0


def unit_map(values):
    squares = jnp.sum(values * values, axis=0, keepdims=True)
    return values * lax.rsqrt(squares + epsilon)


def fill_filters(query_taps, db_taps, filter_query, filter_db):
    cells = filter_query.shape[0]
    row = lax.broadcasted_iota(jnp.int32, (cells, cells), 0)
    col = lax.broadcasted_iota(jnp.int32, (cells, cells), 1)
    down = (col >> 4) - (row >> 4)
    across = (col & (GRID - 1)) - (row & (GRID - 1))
    near = (jnp.abs(down) <= 1) & (jnp.abs(across) <= 1)
    tap = jnp.where(near, down * 3 + across + 4, -1)
    query_matrix = jnp.zeros((cells, cells), jnp.float32)
    db_matrix = jnp.zeros((cells, cells), jnp.float32)
    query_values = query_taps[...].astype(jnp.float32)
    db_values = db_taps[...].astype(jnp.float32)
    for i in range(3):
        for j in range(3):
            hit = tap == 3 * i + j
            back = tap == 8 - (3 * i + j)
            query_matrix = jnp.where(hit, query_values[i : i + 1, j : j + 1], query_matrix)
            db_matrix = jnp.where(back, db_values[i : i + 1, j : j + 1], db_matrix)
    filter_query[...] = query_matrix.astype(jnp.bfloat16)
    filter_db[...] = db_matrix.astype(jnp.bfloat16)


def shortlist_info(ids, image_count, count):
    entries = ids.shape[1]
    shard = jnp.zeros_like(ids)
    for s in range(1, count):
        shard = shard + jnp.where(ids >= s * image_count, 1, 0)
    slot = ids - shard * image_count
    across = jnp.broadcast_to(shard, (entries, entries))
    above = lax.broadcasted_iota(jnp.int32, (entries, entries), 0)
    beside = lax.broadcasted_iota(jnp.int32, (entries, entries), 1)
    earlier = (across.T == across) & (above < beside)
    bucket = jnp.sum(jnp.where(earlier, 1, 0), axis=0, keepdims=True)
    rank = lax.broadcasted_iota(jnp.int32, (TAIL, entries), 0)
    return jnp.where(rank == 0, shard, jnp.where(rank == 1, slot, bucket))


def descending(row):
    entries = row.shape[1]
    across = jnp.broadcast_to(row, (entries, entries))
    down = across.T
    above = lax.broadcasted_iota(jnp.int32, (entries, entries), 0)
    beside = lax.broadcasted_iota(jnp.int32, (entries, entries), 1)
    ahead = (down > across) | ((down == across) & (above < beside))
    rank = jnp.sum(jnp.where(ahead, 1.0, 0.0), axis=0, keepdims=True)
    rank_down = jnp.broadcast_to(rank, (entries, entries)).T
    chosen = jnp.where(rank_down == beside.astype(jnp.float32), down, 0.0)
    return jnp.sum(chosen, axis=0, keepdims=True)


def flip(a, b, size):
    total = 0
    bit = 1
    while bit < size:
        total = total + lax.rem(a // bit + b // bit, 2) * bit
        bit *= 2
    return total


def combo_order(side, line):
    ranked = []
    for j in range(line):
        arrival = 0 if j == 0 else (26 if j == 1 else 40 + 10 * j)
        for u in range(side):
            for v in range(side):
                late = 1000 if j == 0 and u > 0 and v > 0 else 0
                key = arrival + 25 * min(u, 1) + 30 * min(v, 1) + late
                ranked.append((key, (j * side + u) * side + v))
    return [code for _, code in sorted(ranked)]


def kernel(
    db_count,
    pb_count,
    width,
    query_any,
    shortlist_ref,
    database_ref,
    query_taps,
    db_taps,
    out_ref,
    sorted_ref,
    filter_query,
    filter_db,
    raw,
    positive,
    maps,
    info,
    units,
    slot_rows,
    slot_table,
    peaks,
    found,
    returned,
    query_ref,
    map_send,
    map_recv,
    back_send,
    back_recv,
    slot_sem,
    raw_sem,
    query_sem,
):
    count = db_count * pb_count
    chips = db_count // 2
    side = math.isqrt(chips)
    combos = pb_count * chips
    order = combo_order(side, pb_count)
    image_count = database_ref.shape[0]
    cells = units.shape[2]
    db = lax.axis_index("db")
    pb = lax.axis_index("pb")
    chip = db // 2
    core = lax.rem(db, 2)
    me = db * pb_count + pb
    partner = (chip * 2 + 1 - core, pb)
    first_stride = 1 + core * (side - 1)
    second_stride = side - core * (side - 1)

    first_base = pb_count - 1
    second_base = first_base + pb_count * (side - 1)
    partner_base = second_base + pb_count * side * (side - 1)
    sends = partner_base + combos

    def place(index):
        return (index // pb_count, lax.rem(index, pb_count))

    def line_peer(j):
        return (db, flip(pb, j, pb_count))

    def first_peer(u):
        return (flip(chip, u * first_stride, chips) * 2 + core, pb)

    def second_peer(v):
        return (flip(chip, v * second_stride, chips) * 2 + core, pb)

    def map_copy(source, send_slot, device):
        return pltpu.make_async_remote_copy(
            src_ref=maps.at[source],
            dst_ref=maps.at[source],
            send_sem=map_send.at[send_slot],
            recv_sem=map_recv.at[source],
            device_id=device,
            device_id_type=MESH,
        )

    def send_first(source, j):
        for u in range(1, side):
            map_copy(source, first_base + j * (side - 1) + u - 1, first_peer(u)).start()

    def send_second(source, j, u):
        for v in range(1, side):
            slot = second_base + (j * side + u) * (side - 1) + v - 1
            map_copy(source, slot, second_peer(v)).start()

    def back_copy(source, landed):
        return pltpu.make_async_remote_copy(
            src_ref=found.at[source],
            dst_ref=returned.at[landed],
            send_sem=back_send.at[source],
            recv_sem=back_recv.at[landed],
            device_id=place(source),
            device_id_type=MESH,
        )

    def raw_copy(image):
        return pltpu.make_async_copy(database_ref.at[image], raw.at[image], raw_sem.at[image])

    def slot_copy(parity):
        return pltpu.make_async_copy(
            slot_rows.at[parity], slot_table.at[parity], slot_sem.at[parity]
        )

    barrier = pltpu.get_barrier_semaphore()
    peers = [line_peer(j) for j in range(1, pb_count)]
    peers += [first_peer(u) for u in range(1, side)]
    peers += [second_peer(v) for v in range(1, side)]
    peers += [partner]
    for peer in peers:
        pl.semaphore_signal(barrier, inc=1, device_id=peer, device_id_type=MESH)

    query_copy = pltpu.make_async_copy(query_any.at[0], query_ref, query_sem)
    query_copy.start()

    @pl.loop(0, image_count)
    def _(image):
        raw_copy(image).start()

    my_info = shortlist_info(shortlist_ref[...], image_count, count)
    info[...] = my_info
    entries = my_info.shape[1]
    maps[me, cells : cells + TAIL, 0:entries] = my_info.astype(jnp.float32).astype(jnp.bfloat16)
    if maps.shape[2] > entries:
        maps[me, cells : cells + TAIL, entries:] = jnp.zeros(
            (TAIL, maps.shape[2] - entries), jnp.bfloat16
        )
    query_copy.wait()
    maps[me, 0:cells, :] = unit_map(query_ref[...].astype(jnp.float32)).T.astype(jnp.bfloat16)
    rank = lax.broadcasted_iota(jnp.int32, (ROWS, entries), 0)
    rank_value = rank.astype(jnp.float32)
    me_value = jnp.full((ROWS, entries), me, jnp.int32).astype(jnp.float32)

    def normalize(image):
        raw_copy(image).wait()
        units[image] = unit_map(raw[image].astype(jnp.float32)).astype(jnp.bfloat16)

    early = image_count // EARLY
    pl.loop(0, early)(normalize)
    pl.semaphore_wait(barrier, len(peers))

    send_first(me, 0)
    for j in range(1, pb_count):
        map_copy(me, j - 1, line_peer(j)).start()
    map_copy(me, partner_base, partner).start()

    fill_filters(query_taps, db_taps, filter_query, filter_db)
    peaks[...] = jnp.zeros_like(peaks)
    pl.loop(early, image_count)(normalize)

    def decode(turn):
        last = 2 * combos - 1
        odd = lax.rem(turn, 2)
        mid = jnp.where(odd == 1, (turn + 1) // 2, turn // 2 - 1)
        index = jnp.where(turn < 2, 0, jnp.where(turn == 2, 1, mid))
        index = jnp.where(turn == last, combos - 1, index)
        half = jnp.where((turn == 1) | (turn == last), 1, jnp.where(turn < 4, 0, 1 - odd))
        code = 0
        for n in range(combos):
            code = jnp.where(index == n, order[n], code)
        j = code // chips
        u = lax.rem(code // side, side)
        v = lax.rem(code, side)
        owner = lax.rem(core + half, 2)
        offset = u * (1 + owner * (side - 1)) + v * (side - owner * (side - 1))
        other_chip = flip(chip, offset, chips)
        source = (other_chip * 2 + owner) * pb_count + flip(pb, j, pb_count)
        return half, code, j, u, v, source

    def load_slots(source, parity):
        tail = maps[source, cells : cells + TAIL, 0:entries].astype(jnp.float32)
        hit = (tail[0:1, :] == me_value) & (tail[2:3, :] == rank_value)
        slot = jnp.sum(jnp.where(hit, tail[1:2, :], 0.0), axis=1, keepdims=True)
        slot_rows[parity] = jnp.broadcast_to(slot, (ROWS, entries)).astype(jnp.int32)
        slot_copy(parity).start()

    def serve(turn, half, code, j, u, v, source):
        map_copy(source, 0, partner).wait_recv()

        @pl.when(half == 0)
        def _():
            map_copy(source, partner_base + code, partner).start()

            @pl.when((u == 0) & (v == 0))
            def _():
                send_first(source, j)

            @pl.when(v == 0)
            def _():
                send_second(source, j, u)

        @pl.when(turn == 1)
        def _():
            send_second(me, 0, 0)

    load_slots(me, 0)

    def step(ahead, turn, source):
        parity = lax.rem(turn, 2)
        coming = decode(turn + 1)
        upcoming = coming[-1]

        if ahead:

            @pl.when(turn + 1 < 2 * combos)
            def _():
                serve(turn + 1, *coming)

        slot_copy(parity).wait()
        if ahead:
            load_slots(upcoming, 1 - parity)
        for k in range(width):
            slot = jnp.clip(slot_table[parity, k, 0], 0, image_count - 1)
            correlation = jnp.dot(
                maps[source, 0:cells, :], units[slot], preferred_element_type=jnp.float32
            )
            positive[k] = jnp.maximum(correlation, 0.0).astype(jnp.bfloat16)
        for k in range(width):
            rectified = positive[k]
            filtered = jnp.dot(
                filter_query[...], rectified, preferred_element_type=jnp.float32
            ) + jnp.dot(rectified, filter_db[...], preferred_element_type=jnp.float32)
            peaks[k : k + 1, :] = jnp.max(filtered, axis=0, keepdims=True)
        best = peaks[...]
        total = jnp.sum(best, axis=1, keepdims=True) * (score_scale / best.shape[1])
        found[source] = jnp.broadcast_to(total, (ROWS, LANES))

        @pl.when(source != me)
        def _():
            back_copy(source, me).start()

        if not ahead:
            serve(turn + 1, *coming)
            load_slots(upcoming, 1 - parity)
        return upcoming

    source = lax.fori_loop(0, 3, functools.partial(step, False), me)
    lax.fori_loop(3, 2 * combos, functools.partial(step, True), source)
    slot_copy(0).wait()

    returned[me] = found[me]

    @pl.loop(1, count)
    def _(step):
        other = lax.rem(me + step, count)
        back_copy(other, other).wait_recv()

    my_shard = info[0:1, :]
    my_bucket = info[2:3, :]
    scores = jnp.zeros((ROWS, LANES), jnp.float32)
    for s in range(count):
        scores = scores + jnp.where((my_shard == s) & (my_bucket == rank), returned[s], 0.0)
    final = jnp.sum(scores, axis=0, keepdims=True)
    out_ref[...] = final
    sorted_ref[...] = descending(final)

    @pl.loop(1, count)
    def _(step):
        back_copy(lax.rem(me + step, count), me).wait_send()

    @pl.loop(0, sends)
    def _(slot):
        map_copy(me, slot, partner).wait_send()


def body(db_count, pb_count, query_maps, database, shortlist, kernel_query, kernel_db):
    count = db_count * pb_count
    chips = db_count // 2
    side = math.isqrt(chips)
    sends = pb_count - 1 + pb_count * (side - 1) * (1 + side) + pb_count * chips
    image_count, channels, cells = database.shape
    entries = shortlist.shape[1]
    width = 2 * entries // count
    vmem = pl.BlockSpec(memory_space=pltpu.VMEM)
    whole = pl.BlockSpec(memory_space=pl.ANY)
    row = jax.ShapeDtypeStruct((1, entries), jnp.float32)
    scores, ordered = pl.pallas_call(
        functools.partial(kernel, db_count, pb_count, width),
        out_shape=(row, row),
        in_specs=[whole, vmem, whole, vmem, vmem],
        out_specs=(vmem, vmem),
        scratch_shapes=[
            pltpu.VMEM((cells, cells), jnp.bfloat16),
            pltpu.VMEM((cells, cells), jnp.bfloat16),
            pltpu.VMEM((image_count, channels, cells), jnp.bfloat16),
            pltpu.VMEM((width, cells, cells), jnp.bfloat16),
            pltpu.VMEM((count, cells + TAIL, channels), jnp.bfloat16),
            pltpu.VMEM((TAIL, entries), jnp.int32),
            pltpu.VMEM((image_count, channels, cells), jnp.bfloat16),
            pltpu.VMEM((2, ROWS, entries), jnp.int32),
            pltpu.SMEM((2, ROWS, entries), jnp.int32),
            pltpu.VMEM((ROWS, cells), jnp.float32),
            pltpu.VMEM((count, ROWS, LANES), jnp.float32),
            pltpu.VMEM((count, ROWS, LANES), jnp.float32),
            pltpu.VMEM((channels, cells), jnp.bfloat16),
            pltpu.SemaphoreType.DMA((sends,)),
            pltpu.SemaphoreType.DMA((count,)),
            pltpu.SemaphoreType.DMA((count,)),
            pltpu.SemaphoreType.DMA((count,)),
            pltpu.SemaphoreType.DMA((2,)),
            pltpu.SemaphoreType.DMA((image_count,)),
            pltpu.SemaphoreType.DMA,
        ],
        compiler_params=pltpu.CompilerParams(
            collective_id=0, has_side_effects=True, vmem_limit_bytes=56 * 1024 * 1024
        ),
    )(query_maps, shortlist, database, kernel_query, kernel_db)
    return (scores, ordered[:, :TOPK])


def solution(mesh):
    in_specs = (
        P(("db", "pb"), None, None),
        P(("db", "pb"), None, None),
        P(("db", "pb"), None),
        P(),
        P(),
    )
    out_specs = (P(("db", "pb"), None), P(("db", "pb"), None))
    step = functools.partial(body, mesh.shape["db"], mesh.shape["pb"])
    return jax.shard_map(step, mesh=mesh, in_specs=in_specs, out_specs=out_specs, check_vma=False)
```

```python
import functools
import math

import jax
import jax.numpy as jnp
from jax import lax
from jax.experimental import pallas as pl
from jax.experimental.pallas import tpu as pltpu
from jax.sharding import PartitionSpec as P

GRID = 16
TOPK = 100
LANES = 128
ROWS = 8
TAIL = 16
EARLY = 8
MESH = pl.DeviceIdType.MESH

epsilon = 1e-06
score_scale = 8.0


def unit_map(values):
    squares = jnp.sum(values * values, axis=0, keepdims=True)
    return values * lax.rsqrt(squares + epsilon)


def fill_filters(query_taps, db_taps, filter_query, filter_db):
    cells = filter_query.shape[0]
    row = lax.broadcasted_iota(jnp.int32, (cells, cells), 0)
    col = lax.broadcasted_iota(jnp.int32, (cells, cells), 1)
    down = (col >> 4) - (row >> 4)
    across = (col & (GRID - 1)) - (row & (GRID - 1))
    near = (jnp.abs(down) <= 1) & (jnp.abs(across) <= 1)
    tap = jnp.where(near, down * 3 + across + 4, -1)
    query_matrix = jnp.zeros((cells, cells), jnp.float32)
    db_matrix = jnp.zeros((cells, cells), jnp.float32)
    query_values = query_taps[...].astype(jnp.float32)
    db_values = db_taps[...].astype(jnp.float32)
    for i in range(3):
        for j in range(3):
            hit = tap == 3 * i + j
            back = tap == 8 - (3 * i + j)
            query_matrix = jnp.where(hit, query_values[i : i + 1, j : j + 1], query_matrix)
            db_matrix = jnp.where(back, db_values[i : i + 1, j : j + 1], db_matrix)
    filter_query[...] = query_matrix.astype(jnp.bfloat16)
    filter_db[...] = db_matrix.astype(jnp.bfloat16)


def shortlist_info(ids, image_count, count):
    entries = ids.shape[1]
    shard = jnp.zeros_like(ids)
    for s in range(1, count):
        shard = shard + jnp.where(ids >= s * image_count, 1, 0)
    slot = ids - shard * image_count
    across = jnp.broadcast_to(shard, (entries, entries))
    above = lax.broadcasted_iota(jnp.int32, (entries, entries), 0)
    beside = lax.broadcasted_iota(jnp.int32, (entries, entries), 1)
    earlier = (across.T == across) & (above < beside)
    bucket = jnp.sum(jnp.where(earlier, 1, 0), axis=0, keepdims=True)
    rank = lax.broadcasted_iota(jnp.int32, (TAIL, entries), 0)
    return jnp.where(rank == 0, shard, jnp.where(rank == 1, slot, bucket))


def descending(row):
    entries = row.shape[1]
    across = jnp.broadcast_to(row, (entries, entries))
    down = across.T
    above = lax.broadcasted_iota(jnp.int32, (entries, entries), 0)
    beside = lax.broadcasted_iota(jnp.int32, (entries, entries), 1)
    ahead = (down > across) | ((down == across) & (above < beside))
    rank = jnp.sum(jnp.where(ahead, 1.0, 0.0), axis=0, keepdims=True)
    rank_down = jnp.broadcast_to(rank, (entries, entries)).T
    chosen = jnp.where(rank_down == beside.astype(jnp.float32), down, 0.0)
    return jnp.sum(chosen, axis=0, keepdims=True)


def flip(a, b, size):
    total = 0
    bit = 1
    while bit < size:
        total = total + lax.rem(a // bit + b // bit, 2) * bit
        bit *= 2
    return total


def combo_order(side, line):
    ranked = []
    for j in range(line):
        arrival = 0 if j == 0 else (26 if j == 1 else 40 + 10 * j)
        for u in range(side):
            for v in range(side):
                late = 1000 if j == 0 and u > 0 and v > 0 else 0
                key = arrival + 25 * min(u, 1) + 30 * min(v, 1) + late
                ranked.append((key, (j * side + u) * side + v))
    return [code for _, code in sorted(ranked)]


def kernel(
    db_count,
    pb_count,
    width,
    query_any,
    shortlist_ref,
    database_ref,
    query_taps,
    db_taps,
    out_ref,
    sorted_ref,
    filter_query,
    filter_db,
    raw,
    positive,
    maps,
    info,
    units,
    slot_rows,
    slot_table,
    peaks,
    found,
    returned,
    query_ref,
    map_send,
    map_recv,
    back_send,
    back_recv,
    slot_sem,
    raw_sem,
    query_sem,
):
    count = db_count * pb_count
    chips = db_count // 2
    side = math.isqrt(chips)
    combos = pb_count * chips
    order = combo_order(side, pb_count)
    image_count = database_ref.shape[0]
    cells = units.shape[2]
    db = lax.axis_index("db")
    pb = lax.axis_index("pb")
    chip = db // 2
    core = lax.rem(db, 2)
    me = db * pb_count + pb
    partner = (chip * 2 + 1 - core, pb)
    first_stride = 1 + core * (side - 1)
    second_stride = side - core * (side - 1)

    first_base = pb_count - 1
    second_base = first_base + pb_count * (side - 1)
    partner_base = second_base + pb_count * side * (side - 1)
    sends = partner_base + combos

    def place(index):
        return (index // pb_count, lax.rem(index, pb_count))

    def line_peer(j):
        return (db, flip(pb, j, pb_count))

    def first_peer(u):
        return (flip(chip, u * first_stride, chips) * 2 + core, pb)

    def second_peer(v):
        return (flip(chip, v * second_stride, chips) * 2 + core, pb)

    def map_copy(source, send_slot, device):
        return pltpu.make_async_remote_copy(
            src_ref=maps.at[source],
            dst_ref=maps.at[source],
            send_sem=map_send.at[send_slot],
            recv_sem=map_recv.at[source],
            device_id=device,
            device_id_type=MESH,
        )

    def send_first(source, j):
        for u in range(1, side):
            map_copy(source, first_base + j * (side - 1) + u - 1, first_peer(u)).start()

    def send_second(source, j, u):
        for v in range(1, side):
            slot = second_base + (j * side + u) * (side - 1) + v - 1
            map_copy(source, slot, second_peer(v)).start()

    def back_copy(source, landed):
        return pltpu.make_async_remote_copy(
            src_ref=found.at[source],
            dst_ref=returned.at[landed],
            send_sem=back_send.at[source],
            recv_sem=back_recv.at[landed],
            device_id=place(source),
            device_id_type=MESH,
        )

    def raw_copy(image):
        return pltpu.make_async_copy(database_ref.at[image], raw.at[image], raw_sem.at[image])

    def slot_copy(parity):
        return pltpu.make_async_copy(
            slot_rows.at[parity], slot_table.at[parity], slot_sem.at[parity]
        )

    barrier = pltpu.get_barrier_semaphore()
    peers = [line_peer(j) for j in range(1, pb_count)]
    peers += [first_peer(u) for u in range(1, side)]
    peers += [second_peer(v) for v in range(1, side)]
    peers += [partner]
    for peer in peers:
        pl.semaphore_signal(barrier, inc=1, device_id=peer, device_id_type=MESH)

    query_copy = pltpu.make_async_copy(query_any.at[0], query_ref, query_sem)
    query_copy.start()

    @pl.loop(0, image_count)
    def _(image):
        raw_copy(image).start()

    my_info = shortlist_info(shortlist_ref[...], image_count, count)
    info[...] = my_info
    entries = my_info.shape[1]
    maps[me, cells : cells + TAIL, 0:entries] = my_info.astype(jnp.float32).astype(jnp.bfloat16)
    if maps.shape[2] > entries:
        maps[me, cells : cells + TAIL, entries:] = jnp.zeros(
            (TAIL, maps.shape[2] - entries), jnp.bfloat16
        )
    query_copy.wait()
    maps[me, 0:cells, :] = unit_map(query_ref[...].astype(jnp.float32)).T.astype(jnp.bfloat16)
    rank = lax.broadcasted_iota(jnp.int32, (ROWS, entries), 0)
    rank_value = rank.astype(jnp.float32)
    me_value = jnp.full((ROWS, entries), me, jnp.int32).astype(jnp.float32)

    def normalize(image):
        raw_copy(image).wait()
        units[image] = unit_map(raw[image].astype(jnp.float32)).astype(jnp.bfloat16)

    early = image_count // EARLY
    pl.loop(0, early)(normalize)
    pl.semaphore_wait(barrier, len(peers))

    send_first(me, 0)
    for j in range(1, pb_count):
        map_copy(me, j - 1, line_peer(j)).start()
    map_copy(me, partner_base, partner).start()

    fill_filters(query_taps, db_taps, filter_query, filter_db)
    peaks[...] = jnp.zeros_like(peaks)
    pl.loop(early, image_count)(normalize)

    def decode(turn):
        last = 2 * combos - 1
        odd = lax.rem(turn, 2)
        mid = jnp.where(odd == 1, (turn + 1) // 2, turn // 2 - 1)
        index = jnp.where(turn < 2, 0, jnp.where(turn == 2, 1, mid))
        index = jnp.where(turn == last, combos - 1, index)
        half = jnp.where((turn == 1) | (turn == last), 1, jnp.where(turn < 4, 0, 1 - odd))
        code = 0
        for n in range(combos):
            code = jnp.where(index == n, order[n], code)
        j = code // chips
        u = lax.rem(code // side, side)
        v = lax.rem(code, side)
        owner = lax.rem(core + half, 2)
        offset = u * (1 + owner * (side - 1)) + v * (side - owner * (side - 1))
        other_chip = flip(chip, offset, chips)
        source = (other_chip * 2 + owner) * pb_count + flip(pb, j, pb_count)
        return half, code, j, u, v, source

    def load_slots(source, parity):
        tail = maps[source, cells : cells + TAIL, 0:entries].astype(jnp.float32)
        hit = (tail[0:1, :] == me_value) & (tail[2:3, :] == rank_value)
        slot = jnp.sum(jnp.where(hit, tail[1:2, :], 0.0), axis=1, keepdims=True)
        slot_rows[parity] = jnp.broadcast_to(slot, (ROWS, entries)).astype(jnp.int32)
        slot_copy(parity).start()

    def serve(turn, half, code, j, u, v, source):
        map_copy(source, 0, partner).wait_recv()

        @pl.when(half == 0)
        def _():
            map_copy(source, partner_base + code, partner).start()

            @pl.when((u == 0) & (v == 0))
            def _():
                send_first(source, j)

            @pl.when(v == 0)
            def _():
                send_second(source, j, u)

        @pl.when(turn == 1)
        def _():
            send_second(me, 0, 0)

    load_slots(me, 0)

    def step(ahead, turn, source):
        parity = lax.rem(turn, 2)
        coming = decode(turn + 1)
        upcoming = coming[-1]

        if ahead:

            @pl.when(turn + 1 < 2 * combos)
            def _():
                serve(turn + 1, *coming)

        slot_copy(parity).wait()
        if ahead:
            load_slots(upcoming, 1 - parity)
        for k in range(width):
            slot = jnp.clip(slot_table[parity, k, 0], 0, image_count - 1)
            correlation = jnp.dot(
                maps[source, 0:cells, :], units[slot], preferred_element_type=jnp.float32
            )
            positive[k] = jnp.maximum(correlation, 0.0).astype(jnp.bfloat16)
        for k in range(width):
            rectified = positive[k]
            filtered = jnp.dot(
                filter_query[...], rectified, preferred_element_type=jnp.float32
            ) + jnp.dot(rectified, filter_db[...], preferred_element_type=jnp.float32)
            peaks[k : k + 1, :] = jnp.max(filtered, axis=0, keepdims=True)
        best = peaks[...]
        total = jnp.sum(best, axis=1, keepdims=True) * (score_scale / best.shape[1])
        found[source] = jnp.broadcast_to(total, (ROWS, LANES))

        @pl.when(source != me)
        def _():
            back_copy(source, me).start()

        if not ahead:
            serve(turn + 1, *coming)
            load_slots(upcoming, 1 - parity)
        return upcoming

    source = lax.fori_loop(0, 3, functools.partial(step, False), me)
    lax.fori_loop(3, 2 * combos, functools.partial(step, True), source)
    slot_copy(0).wait()

    returned[me] = found[me]

    @pl.loop(1, count)
    def _(step):
        other = lax.rem(me + step, count)
        back_copy(other, other).wait_recv()

    my_shard = info[0:1, :]
    my_bucket = info[2:3, :]
    scores = jnp.zeros((ROWS, LANES), jnp.float32)
    for s in range(count):
        scores = scores + jnp.where((my_shard == s) & (my_bucket == rank), returned[s], 0.0)
    final = jnp.sum(scores, axis=0, keepdims=True)
    out_ref[...] = final
    sorted_ref[...] = descending(final)

    @pl.loop(1, count)
    def _(step):
        back_copy(lax.rem(me + step, count), me).wait_send()

    @pl.loop(0, sends)
    def _(slot):
        map_copy(me, slot, partner).wait_send()


def body(db_count, pb_count, query_maps, database, shortlist, kernel_query, kernel_db):
    count = db_count * pb_count
    chips = db_count // 2
    side = math.isqrt(chips)
    sends = pb_count - 1 + pb_count * (side - 1) * (1 + side) + pb_count * chips
    image_count, channels, cells = database.shape
    entries = shortlist.shape[1]
    width = 2 * entries // count
    vmem = pl.BlockSpec(memory_space=pltpu.VMEM)
    whole = pl.BlockSpec(memory_space=pl.ANY)
    row = jax.ShapeDtypeStruct((1, entries), jnp.float32)
    scores, ordered = pl.pallas_call(
        functools.partial(kernel, db_count, pb_count, width),
        out_shape=(row, row),
        in_specs=[whole, vmem, whole, vmem, vmem],
        out_specs=(vmem, vmem),
        scratch_shapes=[
            pltpu.VMEM((cells, cells), jnp.bfloat16),
            pltpu.VMEM((cells, cells), jnp.bfloat16),
            pltpu.VMEM((image_count, channels, cells), jnp.bfloat16),
            pltpu.VMEM((width, cells, cells), jnp.bfloat16),
            pltpu.VMEM((count, cells + TAIL, channels), jnp.bfloat16),
            pltpu.VMEM((TAIL, entries), jnp.int32),
            pltpu.VMEM((image_count, channels, cells), jnp.bfloat16),
            pltpu.VMEM((2, ROWS, entries), jnp.int32),
            pltpu.SMEM((2, ROWS, entries), jnp.int32),
            pltpu.VMEM((ROWS, cells), jnp.float32),
            pltpu.VMEM((count, ROWS, LANES), jnp.float32),
            pltpu.VMEM((count, ROWS, LANES), jnp.float32),
            pltpu.VMEM((channels, cells), jnp.bfloat16),
            pltpu.SemaphoreType.DMA((sends,)),
            pltpu.SemaphoreType.DMA((count,)),
            pltpu.SemaphoreType.DMA((count,)),
            pltpu.SemaphoreType.DMA((count,)),
            pltpu.SemaphoreType.DMA((2,)),
            pltpu.SemaphoreType.DMA((image_count,)),
            pltpu.SemaphoreType.DMA,
        ],
        compiler_params=pltpu.CompilerParams(
            collective_id=0, has_side_effects=True, vmem_limit_bytes=56 * 1024 * 1024
        ),
    )(query_maps, shortlist, database, kernel_query, kernel_db)
    return (scores, ordered[:, :TOPK])


def solution(mesh):
    in_specs = (
        P(("db", "pb"), None, None),
        P(("db", "pb"), None, None),
        P(("db", "pb"), None),
        P(),
        P(),
    )
    out_specs = (P(("db", "pb"), None), P(("db", "pb"), None))
    step = functools.partial(body, mesh.shape["db"], mesh.shape["pb"])
    return jax.shard_map(step, mesh=mesh, in_specs=in_specs, out_specs=out_specs, check_vma=False)
```
